32 devices in a mesh: dp: 4 (over y, core), tensor: 8 (over z, x).
Axes of the slice: x: 2, y: 2, z: 4, core: 2. Of those that a mesh axis runs over, the one named last changes fastest.
Arguments:
- mixer_input: bfloat16 [256, 8192], P('dp', 'tensor'), may hold values from -6 to 6
- gate_input: bfloat16 [256, 8192], P('dp', 'tensor'), may hold values from -6 to 6
- conv_state: bfloat16 [256, 3, 8192], P('dp', None, 'tensor'), may hold values from -6 to 6
- conv_weight: float32 [4, 8192], P(None, 'tensor'), may hold values from -3 to 3
- conv_bias: float32 [8192], P('tensor'), may hold values from -0.5 to 0.5
- state_proj: bfloat16 [8192, 288], P('tensor'), may hold values from -0.0625 to 0.0625
- step_proj: bfloat16 [256, 8192], P(None, 'tensor'), may hold values from -0.375 to 0.375
- step_bias: float32 [8192], P('tensor'), may hold values from -3 to 0
- decay_rate: float32 [16, 8192], P(None, 'tensor'), may hold values from 0.5 to 16
- skip_gain: float32 [8192], P('tensor'), may hold values from 0.5 to 1.5
- scan_state: float32 [256, 16, 8192], P('dp', None, 'tensor'), may hold values from -6 to 6
- output_proj: bfloat16 [8192, 4096], P('tensor'), may hold values from -0.09375 to 0.09375
- residual: bfloat16 [256, 4096], P('dp', 'tensor'), may hold values from -6 to 6
- router: bfloat16 [4096, 4], replicated, may hold values from -0.09375 to 0.09375
- expert_ids: int32 [256, 2], P('dp'), may hold values from 0 to 3, all different within a row; in each aligned block of 64 rows (0 to 63, 64 to 127, ...) at most 40 rows name the same one
- active: int32 [256], P('dp'), may hold values 0 or 1
- up_weight: bfloat16 [4, 4096, 14336], P('dp', None, 'tensor'), may hold values from -0.09375 to 0.09375
- down_weight: bfloat16 [4, 14336, 4096], P('dp', 'tensor'), may hold values from -0.0625 to 0.0625
Outputs:
- layer_out: bfloat16 [256, 4096], P('dp', 'tensor')
- state_out: float32 [256, 16, 8192], P('dp', None, 'tensor')
- conv_cache: bfloat16 [256, 3, 8192], P('dp', None, 'tensor')
The draws below stay inside these ranges and needn't reach their ends.
Inputs may be any that keep to these rules, and one draw needn't show every extreme that they name: `expert_ids`: each row names two different experts; within each aligned block of 64 sessions (the sessions of one index of dp) no expert is named by more than 40 rows, a bound that some block reaches.
All inputs are finite; a program needn't handle non-finite values. No bound on the sum of `active` on one device may be relied on, other than what follows from the above.
Results may differ from the reference program's by a relative error of at most 0.02.
Values may be sent and summed in bfloat16 or wider, within the bound.
A program may use at most 128 MiB of HBM per device.

```python
import math
import jax
import jax.numpy as jnp
import numpy as np
from jax import lax

DM = 4096
CH = 8192
NSTATE = 16
DT_RANK = 256
CONV = 4
FF = 14336
SESS_DEV = 64
SESSIONS = 256
CAP = 40
EXPERTS = 4
N_DP = 4
N_TENSOR = 8


def set_ends(drawn, rng, least, largest):
    extent = drawn.shape
    spot = [jax.random.randint(jax.random.fold_in(rng, axis), (), 0, extent[axis]) for axis in range(len(extent))]
    drawn = drawn.at[tuple(spot)].set(least)
    longest = extent.index(max(extent))
    spot[longest] = (spot[longest] + 1) % extent[longest]
    return drawn.at[tuple(spot)].set(largest)


def raised(array, stream_key, source, target, parts, factor):
    owner, partner = [(jnp.arange(array.shape[position]) // (array.shape[position] // parts)).reshape([-1 if axis == position else 1 for axis in range(array.ndim)]) for position in (source, target)]
    chosen = jax.random.permutation(stream_key, parts)[partner]
    strong = (owner == chosen) | (owner == (partner + parts // 2) % parts)
    return jnp.where(strong, factor * array, array)


def level_of(key, extent, cuts, low, largest):
    level, own = 1.0, jax.random.fold_in(key, 6)
    for axis_at, parts in cuts:
        heights = jnp.exp(jax.random.uniform(jax.random.fold_in(own, axis_at), (parts,), jnp.float32, low / len(cuts), largest / len(cuts)))
        level = level * jnp.repeat(heights, extent[axis_at] // parts).reshape([-1 if axis == axis_at else 1 for axis in range(len(extent))])
    return level


def shared_out(key, own, number, rows, count, top, limit, lean):
    sequence = jax.random.permutation(key, count)
    packed, usual = shares(count, rows * top, limit, lean, True), shares(count, rows * top, limit, lean, False)
    places = jnp.arange(count)

    def named(sizes, offset_by):
        used = int((sizes > 0).sum())
        fixed = max(1, used // 4)
        shifted = fixed + (places - fixed + offset_by * (used - fixed)) % max(1, count - fixed)
        return jnp.zeros((count,), jnp.int32).at[sequence[jnp.where(places < fixed, places, shifted)]].set(jnp.asarray(sizes, jnp.int32))

    sizes = jnp.where(number % 4 == 0, named(packed, number // 4), named(usual, number - number // 4 - 1))
    mixed = jax.random.permutation(jax.random.fold_in(own, 3), count)
    giver, receiver = mixed[0:count // 2 * 2:2], mixed[1:count // 2 * 2:2]
    room = jnp.minimum(sizes[giver] - 1, limit - sizes[receiver]) // 2
    room = jnp.where((giver == sequence[0]) | (receiver == sequence[0]) | (sizes[receiver] == 0), 0, jnp.maximum(room, 0))
    shifted = jax.random.randint(jax.random.fold_in(own, 4), (count // 2,), 0, 1 << 20) % (room + 1)
    sizes = sizes.at[giver].add(-shifted).at[receiver].add(shifted)
    members = jnp.searchsorted(jnp.cumsum(sizes), jnp.arange(rows * top), side="right").astype(jnp.int32)
    table = members.reshape(top, rows).T
    table = table[jax.random.permutation(jax.random.fold_in(own, 1), rows)]
    offset_by = jax.random.randint(jax.random.fold_in(own, 2), (rows, 1), 0, top)
    return jnp.take_along_axis(table, (jnp.arange(top)[None, :] + offset_by) % top, axis=1)


def shares(amount, total, reach, slope, full):
    portions = [(1 << 20) // math.isqrt(rank ** slope) + 1 for rank in range(1, amount + 1)]
    largest = reach if full else min(reach, max(-(-total // amount), total * portions[0] // sum(portions)))
    least = 1 if total - largest >= amount - 1 else 0
    counts, spare = [largest] + [least] * (amount - 1), total - largest - least * (amount - 1)
    while spare > 0:
        candidates = [i for i in range(1, amount) if counts[i] < largest] or [i for i in range(1, amount) if counts[i] < reach]
        mass, budget = sum([portions[i] for i in candidates]), spare
        for i in candidates:
            extra = min(reach - counts[i], max(1, budget * portions[i] // mass), spare)
            counts[i] = counts[i] + extra
            spare = spare - extra
    return np.array(counts)


def normal_values(stream_key, shape, scale, reach, cuts=(), kind=jnp.bfloat16):
    entries = scale * jax.random.normal(stream_key, shape, jnp.float32)
    if cuts:
        entries = entries * level_of(stream_key, shape, cuts, -0.22, 0.18)
    return jnp.clip(entries, -reach, reach).astype(kind)


def gaussian_with(stream_key, dims, scale, reach, cuts, heavy, kind=jnp.bfloat16):
    drawn = scale * jax.random.normal(stream_key, dims, jnp.float32)
    if cuts:
        drawn = drawn * level_of(stream_key, dims, cuts, -0.22, 0.18)
    return jnp.clip(raised(drawn, jax.random.fold_in(stream_key, 3), *heavy), -reach, reach).astype(kind)


def setup_inputs(seed: int = 0) -> dict:
    keys = jax.random.split(jax.random.key(seed), 19)
    mixer_input = normal_values(keys[0], (SESSIONS, CH), 1.0, 6.0, ((0, 4), (1, 8)))
    gate_input = normal_values(keys[1], (SESSIONS, CH), 1.0, 6.0, ((0, 4), (1, 8)))
    conv_state = normal_values(keys[2], (SESSIONS, CONV - 1, CH), 1.0, 6.0, ((0, 4), (2, 8)))
    conv_weight = normal_values(keys[3], (CONV, CH), CONV ** -0.5, 3.0, ((1, 8),), jnp.float32)
    conv_bias = jnp.clip(jax.random.uniform(keys[4], (CH,), jnp.float32, -0.5, 0.5) * level_of(keys[4], (CH,), ((0, 8),), -0.4, 0.0), -0.5, 0.5)
    state_proj = normal_values(keys[5], (CH, DT_RANK + 2 * NSTATE), CH ** -0.5, 0.0625, ((0, 8),))
    step_proj = normal_values(keys[6], (DT_RANK, CH), DT_RANK ** -0.5, 0.375, ((1, 8),))
    step_bias = jnp.clip(-3.0 + 3.0 * jax.random.uniform(keys[7], (CH,), jnp.float32) ** level_of(keys[7], (CH,), ((0, 8),), -0.2, 0.2), -3.0, 0.0)
    decay_rate = jnp.clip(jnp.exp(math.log(16.0) - 3.465736 * jax.random.uniform(keys[8], (NSTATE, CH), jnp.float32) ** level_of(keys[8], (NSTATE, CH), ((1, 8),), -0.2, 0.2)), 0.5, 16.0)
    skip_gain = jnp.clip(0.5 + 1.0 * jax.random.uniform(keys[9], (CH,), jnp.float32) ** level_of(keys[9], (CH,), ((0, 8),), -0.2, 0.2), 0.5, 1.5)
    scan_state = normal_values(keys[10], (SESSIONS, NSTATE, CH), 1.0, 6.0, ((0, 4), (2, 8)), jnp.float32)
    output_proj = gaussian_with(keys[11], (CH, DM), CH ** -0.5, 0.09375, ((0, 8),), (0, 1, 8, 2.0))
    residual = normal_values(keys[12], (SESSIONS, DM), 1.0, 6.0, ((0, 4), (1, 8)))
    router = normal_values(keys[13], (DM, EXPERTS), DM ** -0.5, 0.09375)
    expert_ids_keys = jax.random.split(jax.random.fold_in(keys[14], 1), SESSIONS // SESS_DEV)
    expert_ids_turns = jax.random.permutation(jax.random.fold_in(keys[14], 3), SESSIONS // SESS_DEV)
    expert_ids = jax.vmap(lambda own, number: shared_out(jax.random.fold_in(keys[14], 2), own, number, SESS_DEV, EXPERTS, 2, CAP, 2))(expert_ids_keys, expert_ids_turns).reshape((SESSIONS, 2))
    active = set_ends((jax.random.randint(keys[15], (SESSIONS,), 0, 4) < 3).astype(jnp.int32), jax.random.fold_in(keys[15], 1), 0, 1)
    up_weight = normal_values(keys[16], (EXPERTS, DM, FF), DM ** -0.5, 0.09375, ((0, 4), (2, 8)))
    down_weight = gaussian_with(keys[17], (EXPERTS, FF, DM), FF ** -0.5, 0.0625, ((0, 4), (1, 8)), (1, 2, 8, 2.0))
    return dict(mixer_input=mixer_input, gate_input=gate_input, conv_state=conv_state, conv_weight=conv_weight, conv_bias=conv_bias, state_proj=state_proj, step_proj=step_proj, step_bias=step_bias, decay_rate=decay_rate, skip_gain=skip_gain, scan_state=scan_state, output_proj=output_proj, residual=residual, router=router, expert_ids=expert_ids, active=active, up_weight=up_weight, down_weight=down_weight)


def reference(mixer_input, gate_input, conv_state, conv_weight, conv_bias, state_proj, step_proj, step_bias, decay_rate, skip_gain, scan_state, output_proj, residual, router, expert_ids, active, up_weight, down_weight):
    window = jnp.concatenate([conv_state, mixer_input[:, None, :]], axis=1)
    conv_sum = lax.optimization_barrier(jnp.sum(window.astype(jnp.float32) * conv_weight[None], axis=1)) + conv_bias
    conv_out = jax.nn.silu(conv_sum).astype(jnp.bfloat16)
    projected = jnp.dot(conv_out, state_proj, preferred_element_type=jnp.float32)
    step_raw = projected[:, :DT_RANK]
    input_map = projected[:, DT_RANK:DT_RANK + NSTATE]
    output_map = projected[:, DT_RANK + NSTATE:]
    step_norm = (step_raw * lax.rsqrt(lax.optimization_barrier(jnp.mean(step_raw * step_raw, axis=1, keepdims=True)) + 1e-06)).astype(jnp.bfloat16)
    step_size = jax.nn.softplus(jnp.dot(step_norm, step_proj, preferred_element_type=jnp.float32) + step_bias)
    conv_float = conv_out.astype(jnp.float32)
    state_next = jnp.exp(-step_size[:, None, :] * decay_rate[None]) * scan_state + (step_size * conv_float)[:, None, :] * input_map[:, :, None]
    live_float = active.astype(jnp.float32)
    live_mask = active == 1
    scan_out = lax.optimization_barrier(jnp.sum(output_map[:, :, None] * state_next, axis=1)) + skip_gain * conv_float
    gated = (scan_out * jax.nn.silu(gate_input.astype(jnp.float32)) * live_float[:, None]).astype(jnp.bfloat16)
    state_out = jnp.where(live_mask[:, None, None], state_next, scan_state)
    conv_cache = jnp.where(live_mask[:, None, None], window[:, 1:, :], conv_state)
    hidden_sum = residual.astype(jnp.float32) + jnp.dot(gated, output_proj, preferred_element_type=jnp.float32)
    inv_rms = lax.rsqrt(lax.optimization_barrier(jnp.sum(hidden_sum * hidden_sum, axis=1)) / DM + 1e-06)
    logits = jnp.dot(hidden_sum, router.astype(jnp.float32), precision=lax.Precision.HIGHEST) * inv_rms[:, None]
    normed = (hidden_sum * inv_rms[:, None]).astype(jnp.bfloat16)
    flat_ids = expert_ids.reshape(N_DP, SESS_DEV * 2)
    one_hot = (flat_ids[:, :, None] == jnp.arange(EXPERTS, dtype=jnp.int32)[None, None, :]).astype(jnp.int32)
    slot_index = lax.optimization_barrier(jnp.sum((jnp.cumsum(one_hot, axis=1) - one_hot) * one_hot, axis=2)).reshape(SESSIONS, 2)
    block_index = jnp.arange(SESSIONS, dtype=jnp.int32) // SESS_DEV
    target_row = block_index[:, None] * CAP + slot_index
    row_numbers = jnp.arange(N_DP * CAP, dtype=jnp.int32)
    block_width = FF // N_TENSOR

    def expert_rows(expert):
        picked = (expert_ids == expert) & live_mask[:, None]
        placement = lax.optimization_barrier(jnp.sum(((target_row[None] == row_numbers[:, None, None]) & picked[None]).astype(jnp.float32), axis=2)).astype(jnp.bfloat16)
        buffer = jnp.dot(placement, normed, preferred_element_type=jnp.float32).astype(jnp.bfloat16)
        hidden = jax.nn.silu(jnp.dot(buffer, up_weight[expert], preferred_element_type=jnp.float32)).astype(jnp.bfloat16)
        hidden_blocks = jnp.transpose(hidden.reshape(N_DP * CAP, N_TENSOR, block_width), (1, 0, 2))
        down_blocks = down_weight[expert].reshape(N_TENSOR, block_width, DM)

        def add_block(total, pieces):
            part = jnp.dot(pieces[0], pieces[1], preferred_element_type=jnp.float32).astype(jnp.bfloat16)
            return (total + part.astype(jnp.float32), None)
        total, unused = lax.scan(add_block, jnp.zeros((N_DP * CAP, DM), jnp.float32), (hidden_blocks, down_blocks))
        return total.astype(jnp.bfloat16)
    results = lax.map(expert_rows, jnp.arange(EXPERTS, dtype=jnp.int32))
    flat_results = results.reshape(EXPERTS * N_DP * CAP, DM)
    gathered = flat_results[expert_ids * (N_DP * CAP) + target_row]
    chosen_logit = jnp.take_along_axis(logits, expert_ids, axis=1)
    first = 1.0 / (1.0 + jnp.exp(chosen_logit[:, 1] - chosen_logit[:, 0]))
    second = 1.0 / (1.0 + jnp.exp(chosen_logit[:, 0] - chosen_logit[:, 1]))
    route_weight = jnp.stack([first, second], axis=1) * live_float[:, None]
    layer_out = (hidden_sum + lax.optimization_barrier(jnp.sum(route_weight[:, :, None] * gathered.astype(jnp.float32), axis=1))).astype(jnp.bfloat16)
    return (layer_out, state_out, conv_cache)
```

```python
import functools

import jax
import jax.numpy as jnp
from jax import lax
from jax.experimental import pallas as pl
from jax.experimental.pallas import tpu as pltpu
from jax.sharding import PartitionSpec as P

DM = 4096
CAP = 40


VMEM = pl.BlockSpec(memory_space=pltpu.VMEM)


def greet(groups):
    barrier = pltpu.get_barrier_semaphore()
    for axis, size in groups:
        me = lax.axis_index(axis)
        for k in range(1, size):
            pl.semaphore_signal(
                barrier,
                inc=1,
                device_id={axis: lax.rem(me + k, size)},
                device_id_type=pl.DeviceIdType.MESH,
            )
    pl.semaphore_wait(barrier, sum(size - 1 for _, size in groups))


def send_all(axis, size, source, target, send_sem, recv_sem):
    me = lax.axis_index(axis)
    copies = []
    for k in range(1, size):
        peer = lax.rem(me + k, size)
        copy = pltpu.make_async_remote_copy(
            src_ref=source(peer, k),
            dst_ref=target(me, k),
            send_sem=send_sem.at[k - 1],
            recv_sem=recv_sem.at[k - 1],
            device_id={axis: peer},
            device_id_type=pl.DeviceIdType.MESH,
        )
        copy.start()
        copies.append(copy)
    return copies


def columns(ref, index, width):
    return ref.at[:, pl.ds(pl.multiple_of(index * width, width), width)]


def sum_rows_kernel(size, x_ref, out_ref, landed, send_a, recv_a, send_b, recv_b):
    me = lax.axis_index("tensor")
    greet((("tensor", size),))
    copies = send_all(
        "tensor",
        size,
        lambda peer, k: x_ref.at[peer],
        lambda mine, k: landed.at[k - 1],
        send_a,
        recv_a,
    )
    total = x_ref[me]
    for k, copy in enumerate(copies):
        copy.wait_recv()
        total += landed[k]
    out_ref[me] = total
    back = send_all(
        "tensor",
        size,
        lambda peer, k: out_ref.at[me],
        lambda mine, k: out_ref.at[mine],
        send_b,
        recv_b,
    )
    for copy in copies:
        copy.wait_send()
    for copy in back:
        copy.wait()


def sum_rows(x, size, collective_id):
    rows, width = x.shape
    chunks = x.reshape(size, rows // size, width)
    out = pl.pallas_call(
        functools.partial(sum_rows_kernel, size),
        out_shape=jax.ShapeDtypeStruct(chunks.shape, x.dtype),
        in_specs=[VMEM],
        out_specs=VMEM,
        scratch_shapes=[pltpu.VMEM((size - 1,) + chunks.shape[1:], x.dtype)]
        + [pltpu.SemaphoreType.DMA((size - 1,))] * 4,
        compiler_params=pltpu.CompilerParams(collective_id=collective_id, has_side_effects=True),
    )(chunks)
    return out.reshape(rows, width)


def sum_columns_kernel(size, x_ref, add_ref, out_ref, landed, total, send_a, recv_a, send_b, recv_b):
    me = lax.axis_index("tensor")
    width = add_ref.shape[1]
    greet((("tensor", size),))
    copies = send_all(
        "tensor",
        size,
        lambda peer, k: columns(x_ref, peer, width),
        lambda mine, k: landed.at[k - 1],
        send_a,
        recv_a,
    )
    total[...] = add_ref[...].astype(jnp.float32) + columns(x_ref, me, width)[...].astype(jnp.float32)
    for k, copy in enumerate(copies):
        copy.wait_recv()
        total[...] += landed[k].astype(jnp.float32)
    columns(out_ref, me, width)[...] = total[...].astype(out_ref.dtype)
    back = send_all(
        "tensor",
        size,
        lambda peer, k: columns(out_ref, me, width),
        lambda mine, k: columns(out_ref, mine, width),
        send_b,
        recv_b,
    )
    for copy in copies:
        copy.wait_send()
    for copy in back:
        copy.wait()


def sum_columns(x, add, size, collective_id):
    rows, width = add.shape
    return pl.pallas_call(
        functools.partial(sum_columns_kernel, size),
        out_shape=jax.ShapeDtypeStruct(x.shape, x.dtype),
        in_specs=[VMEM] * 2,
        out_specs=VMEM,
        scratch_shapes=[
            pltpu.VMEM((size - 1, rows, width), x.dtype),
            pltpu.VMEM((rows, width), jnp.float32),
        ]
        + [pltpu.SemaphoreType.DMA((size - 1,))] * 4,
        compiler_params=pltpu.CompilerParams(collective_id=collective_id, has_side_effects=True),
    )(x, add)


def dispatch_kernel(size, x_ref, out_ref, local_sem, send_sem, recv_sem):
    me = lax.axis_index("dp")
    greet((("dp", size),))
    copies = send_all(
        "dp",
        size,
        lambda peer, k: x_ref.at[peer],
        lambda mine, k: out_ref.at[mine],
        send_sem,
        recv_sem,
    )
    own = pltpu.make_async_copy(x_ref.at[me], out_ref.at[me], local_sem)
    own.start()
    own.wait()
    for copy in copies:
        copy.wait()


def dispatch(x, size, collective_id):
    return pl.pallas_call(
        functools.partial(dispatch_kernel, size),
        out_shape=jax.ShapeDtypeStruct(x.shape, x.dtype),
        in_specs=[VMEM],
        out_specs=VMEM,
        scratch_shapes=[pltpu.SemaphoreType.DMA] + [pltpu.SemaphoreType.DMA((size - 1,))] * 2,
        compiler_params=pltpu.CompilerParams(collective_id=collective_id, has_side_effects=True),
    )(x)


def combine_kernel(size, groups, x_ref, out_ref, landed, total, reply, send_a, recv_a, send_b, recv_b):
    me = lax.axis_index("tensor")
    home = lax.axis_index("dp")
    width = total.shape[1]
    rows = reply.shape[1]
    greet((("tensor", size), ("dp", groups)))
    copies = send_all(
        "tensor",
        size,
        lambda peer, k: columns(x_ref, peer, width),
        lambda mine, k: landed.at[k - 1],
        send_a,
        recv_a,
    )
    total[...] = columns(x_ref, me, width)[...].astype(jnp.float32)
    for k, copy in enumerate(copies):
        copy.wait_recv()
        total[...] += landed[k].astype(jnp.float32)
    for block in range(groups):
        reply[block] = total[block * rows : (block + 1) * rows, :].astype(reply.dtype)
    back = send_all(
        "dp",
        groups,
        lambda peer, k: reply.at[peer],
        lambda mine, k: out_ref.at[mine],
        send_b,
        recv_b,
    )
    out_ref[home] = reply[home]
    for copy in copies:
        copy.wait_send()
    for copy in back:
        copy.wait()


def combine(x, size, groups, collective_id):
    rows, width = x.shape[0] // groups, x.shape[1] // size
    return pl.pallas_call(
        functools.partial(combine_kernel, size, groups),
        out_shape=jax.ShapeDtypeStruct((groups, rows, width), x.dtype),
        in_specs=[VMEM],
        out_specs=VMEM,
        scratch_shapes=[
            pltpu.VMEM((size - 1, x.shape[0], width), x.dtype),
            pltpu.VMEM((x.shape[0], width), jnp.float32),
            pltpu.VMEM((groups, rows, width), x.dtype),
        ]
        + [pltpu.SemaphoreType.DMA((size - 1,))] * 2
        + [pltpu.SemaphoreType.DMA((groups - 1,))] * 2,
        compiler_params=pltpu.CompilerParams(collective_id=collective_id, has_side_effects=True),
    )(x)


def local(
    n_tensor,
    n_dp,
    mixer_input,
    gate_input,
    conv_state,
    conv_weight,
    conv_bias,
    state_proj,
    step_proj,
    step_bias,
    decay_rate,
    skip_gain,
    scan_state,
    output_proj,
    residual,
    router,
    expert_ids,
    active,
    up_weight,
    down_weight,
):
    window = jnp.concatenate([conv_state, mixer_input[:, None, :]], axis=1)
    conv_sum = jnp.sum(window.astype(jnp.float32) * conv_weight[None], axis=1) + conv_bias
    conv_out = jax.nn.silu(conv_sum).astype(jnp.bfloat16)
    partial_proj = jnp.dot(conv_out, state_proj, preferred_element_type=jnp.float32)
    projected = sum_rows(partial_proj, n_tensor, 0)
    low_rank = step_proj.shape[0]
    states = decay_rate.shape[0]
    step_raw = projected[:, :low_rank]
    input_map = projected[:, low_rank : low_rank + states]
    output_map = projected[:, low_rank + states :]
    step_norm = (
        step_raw * lax.rsqrt(jnp.mean(step_raw * step_raw, axis=1, keepdims=True) + 1e-06)
    ).astype(jnp.bfloat16)
    step_size = jax.nn.softplus(
        jnp.dot(step_norm, step_proj, preferred_element_type=jnp.float32) + step_bias
    )
    conv_float = conv_out.astype(jnp.float32)
    state_next = (
        jnp.exp(-step_size[:, None, :] * decay_rate[None]) * scan_state
        + (step_size * conv_float)[:, None, :] * input_map[:, :, None]
    )
    live_float = active.astype(jnp.float32)
    live_mask = active == 1
    scan_out = jnp.sum(output_map[:, :, None] * state_next, axis=1) + skip_gain * conv_float
    gated = (scan_out * jax.nn.silu(gate_input.astype(jnp.float32)) * live_float[:, None]).astype(
        jnp.bfloat16
    )
    state_out = jnp.where(live_mask[:, None, None], state_next, scan_state)
    conv_cache = jnp.where(live_mask[:, None, None], window[:, 1:, :], conv_state)
    experts_total = router.shape[1]
    sessions = expert_ids.shape[0]
    flat_ids = expert_ids.reshape(-1)
    one_hot = (flat_ids[:, None] == jnp.arange(experts_total, dtype=jnp.int32)[None, :]).astype(
        jnp.int32
    )
    slot_index = jnp.sum((jnp.cumsum(one_hot, axis=0) - one_hot) * one_hot, axis=1).reshape(
        sessions, 2
    )
    buffer_row = expert_ids * CAP + slot_index
    row_numbers = jnp.arange(experts_total * CAP, dtype=jnp.int32)
    placement = jnp.sum(
        ((buffer_row[None] == row_numbers[:, None, None]) & live_mask[None, :, None]).astype(
            jnp.float32
        ),
        axis=2,
    ).astype(jnp.bfloat16)
    slice_width = residual.shape[1]
    offset = lax.axis_index("tensor") * slice_width
    up_rows = up_weight[0]
    mixer_part = jnp.dot(gated, output_proj, preferred_element_type=jnp.float32)
    hidden_sum = sum_columns(mixer_part.astype(jnp.bfloat16), residual, n_tensor, 1).astype(
        jnp.float32
    )
    square_sum = jnp.sum(hidden_sum * hidden_sum, axis=1)
    raw_logits = jnp.dot(hidden_sum, router.astype(jnp.float32), precision=lax.Precision.HIGHEST)
    inv_rms = lax.rsqrt(square_sum / DM + 1e-06)
    hidden_local = lax.dynamic_slice_in_dim(hidden_sum, offset, slice_width, 1)
    normed = (hidden_sum * inv_rms[:, None]).astype(jnp.bfloat16)
    outgoing = jnp.dot(placement, normed, preferred_element_type=jnp.float32).astype(jnp.bfloat16)
    outgoing = outgoing.reshape(experts_total, CAP, normed.shape[1])
    incoming = dispatch(outgoing, n_dp, 2)
    up_sum = jnp.dot(
        incoming.reshape(-1, incoming.shape[2]), up_rows, preferred_element_type=jnp.float32
    )
    hidden = jax.nn.silu(up_sum).astype(jnp.bfloat16)
    down_rows = down_weight[0]
    expert_part = jnp.dot(hidden, down_rows, preferred_element_type=jnp.float32)
    returned = combine(expert_part.astype(jnp.bfloat16), n_tensor, n_dp, 3)
    gathered = returned.reshape(-1, slice_width)[buffer_row]
    chosen_logit = jnp.take_along_axis(raw_logits, expert_ids, axis=1) * inv_rms[:, None]
    first = 1.0 / (1.0 + jnp.exp(chosen_logit[:, 1] - chosen_logit[:, 0]))
    second = 1.0 / (1.0 + jnp.exp(chosen_logit[:, 0] - chosen_logit[:, 1]))
    route_weight = jnp.stack([first, second], axis=1) * live_float[:, None]
    layer_out = (
        hidden_local + jnp.sum(route_weight[:, :, None] * gathered.astype(jnp.float32), axis=1)
    ).astype(jnp.bfloat16)
    return (layer_out, state_out, conv_cache)


def solution(mesh):
    placed = (
        P("dp", "tensor"),
        P("dp", "tensor"),
        P("dp", None, "tensor"),
        P(None, "tensor"),
        P("tensor"),
        P("tensor", None),
        P(None, "tensor"),
        P("tensor"),
        P(None, "tensor"),
        P("tensor"),
        P("dp", None, "tensor"),
        P("tensor", None),
        P("dp", "tensor"),
        P(),
        P("dp", None),
        P("dp"),
        P("dp", None, "tensor"),
        P("dp", "tensor", None),
    )
    return jax.shard_map(
        functools.partial(local, mesh.shape["tensor"], mesh.shape["dp"]),
        mesh=mesh,
        in_specs=placed,
        out_specs=(P("dp", "tensor"), P("dp", None, "tensor"), P("dp", None, "tensor")),
        check_vma=False,
    )
```

```python
import functools

import jax
import jax.numpy as jnp
from jax import lax
from jax.experimental import pallas as pl
from jax.experimental.pallas import tpu as pltpu
from jax.sharding import PartitionSpec as P

DM = 4096
CAP = 40


VMEM = pl.BlockSpec(memory_space=pltpu.VMEM)


def greet(groups):
    barrier = pltpu.get_barrier_semaphore()
    for axis, size in groups:
        me = lax.axis_index(axis)
        for k in range(1, size):
            pl.semaphore_signal(
                barrier,
                inc=1,
                device_id={axis: lax.rem(me + k, size)},
                device_id_type=pl.DeviceIdType.MESH,
            )
    pl.semaphore_wait(barrier, sum(size - 1 for _, size in groups))


def send_all(axis, size, source, target, send_sem, recv_sem):
    me = lax.axis_index(axis)
    copies = []
    for k in range(1, size):
        peer = lax.rem(me + k, size)
        copy = pltpu.make_async_remote_copy(
            src_ref=source(peer, k),
            dst_ref=target(me, k),
            send_sem=send_sem.at[k - 1],
            recv_sem=recv_sem.at[k - 1],
            device_id={axis: peer},
            device_id_type=pl.DeviceIdType.MESH,
        )
        copy.start()
        copies.append(copy)
    return copies


def columns(ref, index, width):
    return ref.at[:, pl.ds(pl.multiple_of(index * width, width), width)]


def sum_rows_kernel(size, x_ref, out_ref, landed, send_a, recv_a, send_b, recv_b):
    me = lax.axis_index("tensor")
    greet((("tensor", size),))
    copies = send_all(
        "tensor",
        size,
        lambda peer, k: x_ref.at[peer],
        lambda mine, k: landed.at[k - 1],
        send_a,
        recv_a,
    )
    total = x_ref[me]
    for k, copy in enumerate(copies):
        copy.wait_recv()
        total += landed[k]
    out_ref[me] = total
    back = send_all(
        "tensor",
        size,
        lambda peer, k: out_ref.at[me],
        lambda mine, k: out_ref.at[mine],
        send_b,
        recv_b,
    )
    for copy in copies:
        copy.wait_send()
    for copy in back:
        copy.wait()


def sum_rows(x, size, collective_id):
    rows, width = x.shape
    chunks = x.reshape(size, rows // size, width)
    out = pl.pallas_call(
        functools.partial(sum_rows_kernel, size),
        out_shape=jax.ShapeDtypeStruct(chunks.shape, x.dtype),
        in_specs=[VMEM],
        out_specs=VMEM,
        scratch_shapes=[pltpu.VMEM((size - 1,) + chunks.shape[1:], x.dtype)]
        + [pltpu.SemaphoreType.DMA((size - 1,))] * 4,
        compiler_params=pltpu.CompilerParams(collective_id=collective_id, has_side_effects=True),
    )(chunks)
    return out.reshape(rows, width)


def split(size):
    inner = 2 ** ((size.bit_length() - 1) // 2)
    return (size // inner, inner) if size % inner == 0 else (size, 1)


def remote(source, target, send_sem, recv_sem, peer):
    copy = pltpu.make_async_remote_copy(
        src_ref=source,
        dst_ref=target,
        send_sem=send_sem,
        recv_sem=recv_sem,
        device_id={"tensor": peer},
        device_id_type=pl.DeviceIdType.MESH,
    )
    copy.start()
    return copy


def reduce_scatter(size, produce, own, part, near, mid, far, sems):
    outer, inner = split(size)
    me = lax.axis_index("tensor")
    high, low = me // inner, lax.rem(me, inner)
    near_send, near_recv, far_send, far_recv = sems
    copies = {}
    hops = []

    def pass_on(k):
        for j in range(1, inner):
            copies[k, j].wait_recv()
            own[k] += near[k, j - 1].astype(jnp.float32)
        if k:
            mid[k - 1] = own[k].astype(mid.dtype)
            peer = lax.rem(high + k, outer) * inner + low
            hops.append(
                remote(mid.at[k - 1], far.at[k - 1], far_send.at[k - 1], far_recv.at[k - 1], peer)
            )

    order = list(range(1, outer)) + [0]
    for place, k in enumerate(order):
        row = lax.rem(high + k, outer) * inner
        for j in range(1, inner):
            side = lax.rem(low + j, inner)
            part[k, j - 1] = produce(row + side).astype(part.dtype)
            copies[k, j] = remote(
                part.at[k, j - 1],
                near.at[k, j - 1],
                near_send.at[k, j - 1],
                near_recv.at[k, j - 1],
                high * inner + side,
            )
        own[k] = produce(row + low)
        if place:
            pass_on(order[place - 1])
    pass_on(0)
    for k, hop in enumerate(hops):
        hop.wait_recv()
        own[0] += far[k].astype(jnp.float32)
    return list(copies.values()) + hops


def reduce_scratch(size, rows, width, kind):
    outer, inner = split(size)
    return [
        pltpu.VMEM((outer, rows, width), jnp.float32),
        pltpu.VMEM((outer, inner - 1, rows, width), kind),
        pltpu.VMEM((outer, inner - 1, rows, width), kind),
        pltpu.VMEM((outer - 1, rows, width), kind),
        pltpu.VMEM((outer - 1, rows, width), kind),
    ] + [pltpu.SemaphoreType.DMA((outer, inner - 1))] * 2 + [
        pltpu.SemaphoreType.DMA((outer - 1,))
    ] * 2


def sum_columns_kernel(
    size, x_ref, add_ref, out_ref, own, part, near, mid, far, s0, s1, s2, s3, g0, g1, g2, g3
):
    outer, inner = split(size)
    me = lax.axis_index("tensor")
    high, low = me // inner, lax.rem(me, inner)
    width = add_ref.shape[1]
    greet((("tensor", size),))
    sent = reduce_scatter(
        size,
        lambda t: columns(x_ref, t, width)[...].astype(jnp.float32),
        own,
        part,
        near,
        mid,
        far,
        (s0, s1, s2, s3),
    )
    total = own[0] + add_ref[...].astype(jnp.float32)
    columns(out_ref, me, width)[...] = total.astype(out_ref.dtype)
    block = columns(out_ref, me, width)
    hops = [
        remote(block, block, g0.at[k - 1], g1.at[k - 1], lax.rem(high + k, outer) * inner + low)
        for k in range(1, outer)
    ]

    def spread(k):
        block = columns(out_ref, lax.rem(high + outer - k, outer) * inner + low, width)
        return [
            remote(
                block,
                block,
                g2.at[k, j - 1],
                g3.at[k, j - 1],
                high * inner + lax.rem(low + j, inner),
            )
            for j in range(1, inner)
        ]

    sides = spread(0)
    for k, hop in enumerate(hops):
        hop.wait_recv()
        sides += spread(k + 1)
    for copy in sent + hops:
        copy.wait_send()
    for copy in sides:
        copy.wait()


def sum_columns(x, add, size, collective_id):
    rows, width = add.shape
    outer, inner = split(size)
    return pl.pallas_call(
        functools.partial(sum_columns_kernel, size),
        out_shape=jax.ShapeDtypeStruct(x.shape, x.dtype),
        in_specs=[VMEM] * 2,
        out_specs=VMEM,
        scratch_shapes=reduce_scratch(size, rows, width, x.dtype)
        + [pltpu.SemaphoreType.DMA((outer - 1,))] * 2
        + [pltpu.SemaphoreType.DMA((outer, inner - 1))] * 2,
        compiler_params=pltpu.CompilerParams(collective_id=collective_id, has_side_effects=True),
    )(x, add)


def dispatch_kernel(size, x_ref, out_ref, local_sem, send_sem, recv_sem):
    me = lax.axis_index("dp")
    greet((("dp", size),))
    copies = send_all(
        "dp",
        size,
        lambda peer, k: x_ref.at[peer],
        lambda mine, k: out_ref.at[mine],
        send_sem,
        recv_sem,
    )
    own = pltpu.make_async_copy(x_ref.at[me], out_ref.at[me], local_sem)
    own.start()
    own.wait()
    for copy in copies:
        copy.wait()


def dispatch(x, size, collective_id):
    return pl.pallas_call(
        functools.partial(dispatch_kernel, size),
        out_shape=jax.ShapeDtypeStruct(x.shape, x.dtype),
        in_specs=[VMEM],
        out_specs=VMEM,
        scratch_shapes=[pltpu.SemaphoreType.DMA] + [pltpu.SemaphoreType.DMA((size - 1,))] * 2,
        compiler_params=pltpu.CompilerParams(collective_id=collective_id, has_side_effects=True),
    )(x)


def combine_kernel(
    size, groups, x_ref, w_ref, out_ref, weights, load, reply, b0, b1,
    own, part, near, mid, far, s0, s1, s2, s3
):
    outer, inner = split(size)
    me = lax.axis_index("tensor")
    high, low = me // inner, lax.rem(me, inner)
    home = lax.axis_index("dp")
    rows, width = reply.shape[1:]
    loads = []
    for k in list(range(1, outer)) + [0]:
        for j in list(range(1, inner)) + [0]:
            t = lax.rem(high + k, outer) * inner + lax.rem(low + j, inner)
            place = len(loads)
            loads.append(
                pltpu.make_async_copy(columns(w_ref, t, width), weights.at[place], load.at[place])
            )
            loads[-1].start()
    greet((("tensor", size), ("dp", groups)))
    turn = iter(range(size))

    def produce(t):
        place = next(turn)
        loads[place].wait()
        return jnp.dot(x_ref[...], weights[place], preferred_element_type=jnp.float32).astype(
            x_ref.dtype
        ).astype(jnp.float32)

    sent = reduce_scatter(size, produce, own, part, near, mid, far, (s0, s1, s2, s3))
    for block in range(groups):
        reply[block] = own[0, block * rows : (block + 1) * rows, :].astype(reply.dtype)
    back = send_all(
        "dp",
        groups,
        lambda peer, k: reply.at[peer],
        lambda mine, k: out_ref.at[mine],
        b0,
        b1,
    )
    out_ref[home] = reply[home]
    for copy in sent:
        copy.wait_send()
    for copy in back:
        copy.wait()


def combine(x, w, size, groups, collective_id):
    rows, width = x.shape[0] // groups, w.shape[1] // size
    return pl.pallas_call(
        functools.partial(combine_kernel, size, groups),
        out_shape=jax.ShapeDtypeStruct((groups, rows, width), x.dtype),
        in_specs=[VMEM, pl.BlockSpec(memory_space=pl.ANY)],
        out_specs=VMEM,
        scratch_shapes=[
            pltpu.VMEM((size, w.shape[0], width), w.dtype),
            pltpu.SemaphoreType.DMA((size,)),
            pltpu.VMEM((groups, rows, width), x.dtype),
        ]
        + [pltpu.SemaphoreType.DMA((groups - 1,))] * 2
        + reduce_scratch(size, x.shape[0], width, x.dtype),
        compiler_params=pltpu.CompilerParams(collective_id=collective_id, has_side_effects=True),
    )(x, w)


def local(
    n_tensor,
    n_dp,
    mixer_input,
    gate_input,
    conv_state,
    conv_weight,
    conv_bias,
    state_proj,
    step_proj,
    step_bias,
    decay_rate,
    skip_gain,
    scan_state,
    output_proj,
    residual,
    router,
    expert_ids,
    active,
    up_weight,
    down_weight,
):
    window = jnp.concatenate([conv_state, mixer_input[:, None, :]], axis=1)
    conv_sum = jnp.sum(window.astype(jnp.float32) * conv_weight[None], axis=1) + conv_bias
    conv_out = jax.nn.silu(conv_sum).astype(jnp.bfloat16)
    partial_proj = jnp.dot(conv_out, state_proj, preferred_element_type=jnp.float32)
    projected = sum_rows(partial_proj, n_tensor, 0)
    low_rank = step_proj.shape[0]
    states = decay_rate.shape[0]
    step_raw = projected[:, :low_rank]
    input_map = projected[:, low_rank : low_rank + states]
    output_map = projected[:, low_rank + states :]
    step_norm = (
        step_raw * lax.rsqrt(jnp.mean(step_raw * step_raw, axis=1, keepdims=True) + 1e-06)
    ).astype(jnp.bfloat16)
    step_size = jax.nn.softplus(
        jnp.dot(step_norm, step_proj, preferred_element_type=jnp.float32) + step_bias
    )
    conv_float = conv_out.astype(jnp.float32)
    state_next = (
        jnp.exp(-step_size[:, None, :] * decay_rate[None]) * scan_state
        + (step_size * conv_float)[:, None, :] * input_map[:, :, None]
    )
    live_float = active.astype(jnp.float32)
    live_mask = active == 1
    scan_out = jnp.sum(output_map[:, :, None] * state_next, axis=1) + skip_gain * conv_float
    gated = (scan_out * jax.nn.silu(gate_input.astype(jnp.float32)) * live_float[:, None]).astype(
        jnp.bfloat16
    )
    state_out = jnp.where(live_mask[:, None, None], state_next, scan_state)
    conv_cache = jnp.where(live_mask[:, None, None], window[:, 1:, :], conv_state)
    experts_total = router.shape[1]
    sessions = expert_ids.shape[0]
    flat_ids = expert_ids.reshape(-1)
    one_hot = (flat_ids[:, None] == jnp.arange(experts_total, dtype=jnp.int32)[None, :]).astype(
        jnp.int32
    )
    slot_index = jnp.sum((jnp.cumsum(one_hot, axis=0) - one_hot) * one_hot, axis=1).reshape(
        sessions, 2
    )
    buffer_row = expert_ids * CAP + slot_index
    row_numbers = jnp.arange(experts_total * CAP, dtype=jnp.int32)
    placement = jnp.sum(
        ((buffer_row[None] == row_numbers[:, None, None]) & live_mask[None, :, None]).astype(
            jnp.float32
        ),
        axis=2,
    ).astype(jnp.bfloat16)
    slice_width = residual.shape[1]
    offset = lax.axis_index("tensor") * slice_width
    up_rows = up_weight[0]
    mixer_part = jnp.dot(gated, output_proj, preferred_element_type=jnp.float32)
    hidden_sum = sum_columns(mixer_part.astype(jnp.bfloat16), residual, n_tensor, 1).astype(
        jnp.float32
    )
    square_sum = jnp.sum(hidden_sum * hidden_sum, axis=1)
    raw_logits = jnp.dot(hidden_sum, router.astype(jnp.float32), precision=lax.Precision.HIGHEST)
    inv_rms = lax.rsqrt(square_sum / DM + 1e-06)
    hidden_local = lax.dynamic_slice_in_dim(hidden_sum, offset, slice_width, 1)
    normed = (hidden_sum * inv_rms[:, None]).astype(jnp.bfloat16)
    outgoing = jnp.dot(placement, normed, preferred_element_type=jnp.float32).astype(jnp.bfloat16)
    outgoing = outgoing.reshape(experts_total, CAP, normed.shape[1])
    incoming = dispatch(outgoing, n_dp, 2)
    up_sum = jnp.dot(
        incoming.reshape(-1, incoming.shape[2]), up_rows, preferred_element_type=jnp.float32
    )
    hidden = jax.nn.silu(up_sum).astype(jnp.bfloat16)
    down_rows = down_weight[0]
    returned = combine(hidden, down_rows, n_tensor, n_dp, 3)
    gathered = returned.reshape(-1, slice_width)[buffer_row]
    chosen_logit = jnp.take_along_axis(raw_logits, expert_ids, axis=1) * inv_rms[:, None]
    first = 1.0 / (1.0 + jnp.exp(chosen_logit[:, 1] - chosen_logit[:, 0]))
    second = 1.0 / (1.0 + jnp.exp(chosen_logit[:, 0] - chosen_logit[:, 1]))
    route_weight = jnp.stack([first, second], axis=1) * live_float[:, None]
    layer_out = (
        hidden_local + jnp.sum(route_weight[:, :, None] * gathered.astype(jnp.float32), axis=1)
    ).astype(jnp.bfloat16)
    return (layer_out, state_out, conv_cache)


def solution(mesh):
    placed = (
        P("dp", "tensor"),
        P("dp", "tensor"),
        P("dp", None, "tensor"),
        P(None, "tensor"),
        P("tensor"),
        P("tensor", None),
        P(None, "tensor"),
        P("tensor"),
        P(None, "tensor"),
        P("tensor"),
        P("dp", None, "tensor"),
        P("tensor", None),
        P("dp", "tensor"),
        P(),
        P("dp", None),
        P("dp"),
        P("dp", None, "tensor"),
        P("dp", "tensor", None),
    )
    return jax.shard_map(
        functools.partial(local, mesh.shape["tensor"], mesh.shape["dp"]),
        mesh=mesh,
        in_specs=placed,
        out_specs=(P("dp", "tensor"), P("dp", None, "tensor"), P("dp", None, "tensor")),
        check_vma=False,
    )
```

```python
import functools

import jax
import jax.numpy as jnp
from jax import lax
from jax.experimental import pallas as pl
from jax.experimental.pallas import tpu as pltpu
from jax.sharding import PartitionSpec as P

DM = 4096
CAP = 40


VMEM = pl.BlockSpec(memory_space=pltpu.VMEM)


def greet(groups):
    barrier = pltpu.get_barrier_semaphore()
    for axis, size in groups:
        me = lax.axis_index(axis)
        for k in range(1, size):
            pl.semaphore_signal(
                barrier,
                inc=1,
                device_id={axis: lax.rem(me + k, size)},
                device_id_type=pl.DeviceIdType.MESH,
            )
    pl.semaphore_wait(barrier, sum(size - 1 for _, size in groups))


def send_all(axis, size, source, target, send_sem, recv_sem):
    me = lax.axis_index(axis)
    copies = []
    for k in range(1, size):
        peer = lax.rem(me + k, size)
        copy = pltpu.make_async_remote_copy(
            src_ref=source(peer, k),
            dst_ref=target(me, k),
            send_sem=send_sem.at[k - 1],
            recv_sem=recv_sem.at[k - 1],
            device_id={axis: peer},
            device_id_type=pl.DeviceIdType.MESH,
        )
        copy.start()
        copies.append(copy)
    return copies


def columns(ref, index, width):
    return ref.at[:, pl.ds(pl.multiple_of(index * width, width), width)]


def sum_rows_kernel(size, x_ref, out_ref, landed, send_a, recv_a, send_b, recv_b):
    me = lax.axis_index("tensor")
    greet((("tensor", size),))
    copies = send_all(
        "tensor",
        size,
        lambda peer, k: x_ref.at[peer],
        lambda mine, k: landed.at[k - 1],
        send_a,
        recv_a,
    )
    total = x_ref[me]
    for k, copy in enumerate(copies):
        copy.wait_recv()
        total += landed[k]
    out_ref[me] = total
    back = send_all(
        "tensor",
        size,
        lambda peer, k: out_ref.at[me],
        lambda mine, k: out_ref.at[mine],
        send_b,
        recv_b,
    )
    for copy in copies:
        copy.wait_send()
    for copy in back:
        copy.wait()


def sum_rows(x, size, collective_id):
    rows, width = x.shape
    chunks = x.reshape(size, rows // size, width)
    out = pl.pallas_call(
        functools.partial(sum_rows_kernel, size),
        out_shape=jax.ShapeDtypeStruct(chunks.shape, x.dtype),
        in_specs=[VMEM],
        out_specs=VMEM,
        scratch_shapes=[pltpu.VMEM((size - 1,) + chunks.shape[1:], x.dtype)]
        + [pltpu.SemaphoreType.DMA((size - 1,))] * 4,
        compiler_params=pltpu.CompilerParams(collective_id=collective_id, has_side_effects=True),
    )(chunks)
    return out.reshape(rows, width)


def split(size):
    inner = 2 ** ((size.bit_length() - 1) // 2)
    return (size // inner, inner) if size % inner == 0 else (size, 1)


def remote(source, target, send_sem, recv_sem, peer):
    copy = pltpu.make_async_remote_copy(
        src_ref=source,
        dst_ref=target,
        send_sem=send_sem,
        recv_sem=recv_sem,
        device_id={"tensor": peer},
        device_id_type=pl.DeviceIdType.MESH,
    )
    copy.start()
    return copy


def reduce_scatter(size, produce, own, part, near, mid, far, sems):
    outer, inner = split(size)
    me = lax.axis_index("tensor")
    high, low = me // inner, lax.rem(me, inner)
    near_send, near_recv, far_send, far_recv = sems
    copies = {}
    hops = []

    def pass_on(k):
        for j in range(1, inner):
            copies[k, j].wait_recv()
            own[k] += near[k, j - 1].astype(jnp.float32)
        if k:
            mid[k - 1] = own[k].astype(mid.dtype)
            peer = lax.rem(high + k, outer) * inner + low
            hops.append(
                remote(mid.at[k - 1], far.at[k - 1], far_send.at[k - 1], far_recv.at[k - 1], peer)
            )

    order = list(range(1, outer)) + [0]
    for place, k in enumerate(order):
        row = lax.rem(high + k, outer) * inner
        for j in range(1, inner):
            side = lax.rem(low + j, inner)
            part[k, j - 1] = produce(row + side).astype(part.dtype)
            copies[k, j] = remote(
                part.at[k, j - 1],
                near.at[k, j - 1],
                near_send.at[k, j - 1],
                near_recv.at[k, j - 1],
                high * inner + side,
            )
        own[k] = produce(row + low)
        if place:
            pass_on(order[place - 1])
    pass_on(0)
    for k, hop in enumerate(hops):
        hop.wait_recv()
        own[0] += far[k].astype(jnp.float32)
    return list(copies.values()) + hops


def reduce_scratch(size, rows, width, kind):
    outer, inner = split(size)
    return [
        pltpu.VMEM((outer, rows, width), jnp.float32),
        pltpu.VMEM((outer, inner - 1, rows, width), kind),
        pltpu.VMEM((outer, inner - 1, rows, width), kind),
        pltpu.VMEM((outer - 1, rows, width), kind),
        pltpu.VMEM((outer - 1, rows, width), kind),
    ] + [pltpu.SemaphoreType.DMA((outer, inner - 1))] * 2 + [
        pltpu.SemaphoreType.DMA((outer - 1,))
    ] * 2


def sum_columns_kernel(
    size, x_ref, add_ref, out_ref, own, part, near, mid, far, s0, s1, s2, s3, g0, g1, g2, g3
):
    outer, inner = split(size)
    me = lax.axis_index("tensor")
    high, low = me // inner, lax.rem(me, inner)
    width = add_ref.shape[1]
    greet((("tensor", size),))
    sent = reduce_scatter(
        size,
        lambda t: columns(x_ref, t, width)[...].astype(jnp.float32),
        own,
        part,
        near,
        mid,
        far,
        (s0, s1, s2, s3),
    )
    total = own[0] + add_ref[...].astype(jnp.float32)
    columns(out_ref, me, width)[...] = total.astype(out_ref.dtype)
    block = columns(out_ref, me, width)
    hops = [
        remote(block, block, g0.at[k - 1], g1.at[k - 1], lax.rem(high + k, outer) * inner + low)
        for k in range(1, outer)
    ]

    def spread(k):
        block = columns(out_ref, lax.rem(high + outer - k, outer) * inner + low, width)
        return [
            remote(
                block,
                block,
                g2.at[k, j - 1],
                g3.at[k, j - 1],
                high * inner + lax.rem(low + j, inner),
            )
            for j in range(1, inner)
        ]

    sides = spread(0)
    for k, hop in enumerate(hops):
        hop.wait_recv()
        sides += spread(k + 1)
    for copy in sent + hops:
        copy.wait_send()
    for copy in sides:
        copy.wait()


def sum_columns(x, add, size, collective_id):
    rows, width = add.shape
    outer, inner = split(size)
    return pl.pallas_call(
        functools.partial(sum_columns_kernel, size),
        out_shape=jax.ShapeDtypeStruct(x.shape, x.dtype),
        in_specs=[VMEM] * 2,
        out_specs=VMEM,
        scratch_shapes=reduce_scratch(size, rows, width, x.dtype)
        + [pltpu.SemaphoreType.DMA((outer - 1,))] * 2
        + [pltpu.SemaphoreType.DMA((outer, inner - 1))] * 2,
        compiler_params=pltpu.CompilerParams(collective_id=collective_id, has_side_effects=True),
    )(x, add)


def dispatch_kernel(size, x_ref, out_ref, local_sem, send_sem, recv_sem):
    me = lax.axis_index("dp")
    greet((("dp", size),))
    copies = send_all(
        "dp",
        size,
        lambda peer, k: x_ref.at[peer],
        lambda mine, k: out_ref.at[mine],
        send_sem,
        recv_sem,
    )
    own = pltpu.make_async_copy(x_ref.at[me], out_ref.at[me], local_sem)
    own.start()
    own.wait()
    for copy in copies:
        copy.wait()


def dispatch(x, size, collective_id):
    return pl.pallas_call(
        functools.partial(dispatch_kernel, size),
        out_shape=jax.ShapeDtypeStruct(x.shape, x.dtype),
        in_specs=[VMEM],
        out_specs=VMEM,
        scratch_shapes=[pltpu.SemaphoreType.DMA] + [pltpu.SemaphoreType.DMA((size - 1,))] * 2,
        compiler_params=pltpu.CompilerParams(collective_id=collective_id, has_side_effects=True),
    )(x)


def combine_kernel(
    size, groups, x_ref, w_ref, out_ref, weights, load, reply, b0, b1,
    own, part, near, mid, far, s0, s1, s2, s3
):
    outer, inner = split(size)
    me = lax.axis_index("tensor")
    high, low = me // inner, lax.rem(me, inner)
    home = lax.axis_index("dp")
    rows, width = reply.shape[1:]
    loads = []
    for k in list(range(1, outer)) + [0]:
        for j in list(range(1, inner)) + [0]:
            t = lax.rem(high + k, outer) * inner + lax.rem(low + j, inner)
            place = len(loads)
            loads.append(
                pltpu.make_async_copy(columns(w_ref, t, width), weights.at[place], load.at[place])
            )
            loads[-1].start()
    greet((("tensor", size), ("dp", groups)))
    turn = iter(range(size))

    def produce(t):
        place = next(turn)
        loads[place].wait()
        return jnp.dot(x_ref[...], weights[place], preferred_element_type=jnp.float32).astype(
            x_ref.dtype
        ).astype(jnp.float32)

    sent = reduce_scatter(size, produce, own, part, near, mid, far, (s0, s1, s2, s3))
    for block in range(groups):
        reply[block] = own[0, block * rows : (block + 1) * rows, :].astype(reply.dtype)
    back = send_all(
        "dp",
        groups,
        lambda peer, k: reply.at[peer],
        lambda mine, k: out_ref.at[mine],
        b0,
        b1,
    )
    out_ref[home] = reply[home]
    for copy in sent:
        copy.wait_send()
    for copy in back:
        copy.wait()


def combine(x, w, size, groups, collective_id):
    rows, width = x.shape[0] // groups, w.shape[1] // size
    return pl.pallas_call(
        functools.partial(combine_kernel, size, groups),
        out_shape=jax.ShapeDtypeStruct((groups, rows, width), x.dtype),
        in_specs=[VMEM, pl.BlockSpec(memory_space=pl.ANY)],
        out_specs=VMEM,
        scratch_shapes=[
            pltpu.VMEM((size, w.shape[0], width), w.dtype),
            pltpu.SemaphoreType.DMA((size,)),
            pltpu.VMEM((groups, rows, width), x.dtype),
        ]
        + [pltpu.SemaphoreType.DMA((groups - 1,))] * 2
        + reduce_scratch(size, x.shape[0], width, x.dtype),
        compiler_params=pltpu.CompilerParams(collective_id=collective_id, has_side_effects=True),
    )(x, w)


def local(
    n_tensor,
    n_dp,
    mixer_input,
    gate_input,
    conv_state,
    conv_weight,
    conv_bias,
    state_proj,
    step_proj,
    step_bias,
    decay_rate,
    skip_gain,
    scan_state,
    output_proj,
    residual,
    router,
    expert_ids,
    active,
    up_weight,
    down_weight,
):
    window = jnp.concatenate([conv_state, mixer_input[:, None, :]], axis=1)
    conv_sum = jnp.sum(window.astype(jnp.float32) * conv_weight[None], axis=1) + conv_bias
    conv_out = jax.nn.silu(conv_sum).astype(jnp.bfloat16)
    partial_proj = jnp.dot(conv_out, state_proj, preferred_element_type=jnp.float32)
    projected = sum_rows(partial_proj, n_tensor, 0)
    low_rank = step_proj.shape[0]
    states = decay_rate.shape[0]
    step_raw = projected[:, :low_rank]
    input_map = projected[:, low_rank : low_rank + states]
    output_map = projected[:, low_rank + states :]
    step_norm = (
        step_raw * lax.rsqrt(jnp.mean(step_raw * step_raw, axis=1, keepdims=True) + 1e-06)
    ).astype(jnp.bfloat16)
    step_size = jax.nn.softplus(
        jnp.dot(step_norm, step_proj, preferred_element_type=jnp.float32) + step_bias
    )
    conv_float = conv_out.astype(jnp.float32)
    state_next = (
        jnp.exp(-step_size[:, None, :] * decay_rate[None]) * scan_state
        + (step_size * conv_float)[:, None, :] * input_map[:, :, None]
    )
    live_float = active.astype(jnp.float32)
    live_mask = active == 1
    scan_out = jnp.sum(output_map[:, :, None] * state_next, axis=1) + skip_gain * conv_float
    gated = (scan_out * jax.nn.silu(gate_input.astype(jnp.float32)) * live_float[:, None]).astype(
        jnp.bfloat16
    )
    state_out = jnp.where(live_mask[:, None, None], state_next, scan_state)
    conv_cache = jnp.where(live_mask[:, None, None], window[:, 1:, :], conv_state)
    experts_total = router.shape[1]
    sessions = expert_ids.shape[0]
    flat_ids = expert_ids.reshape(-1)
    one_hot = (flat_ids[:, None] == jnp.arange(experts_total, dtype=jnp.int32)[None, :]).astype(
        jnp.int32
    )
    slot_index = jnp.sum((jnp.cumsum(one_hot, axis=0) - one_hot) * one_hot, axis=1).reshape(
        sessions, 2
    )
    buffer_row = expert_ids * CAP + slot_index
    row_numbers = jnp.arange(experts_total * CAP, dtype=jnp.int32)
    placement = jnp.sum(
        ((buffer_row[None] == row_numbers[:, None, None]) & live_mask[None, :, None]).astype(
            jnp.float32
        ),
        axis=2,
    ).astype(jnp.bfloat16)
    slice_width = residual.shape[1]
    offset = lax.axis_index("tensor") * slice_width
    up_rows = up_weight[0]
    mixer_part = jnp.dot(gated, output_proj, preferred_element_type=jnp.float32)
    hidden_sum = sum_columns(mixer_part.astype(jnp.bfloat16), residual, n_tensor, 1).astype(
        jnp.float32
    )
    square_sum = jnp.sum(hidden_sum * hidden_sum, axis=1)
    raw_logits = jnp.dot(hidden_sum, router.astype(jnp.float32), precision=lax.Precision.HIGHEST)
    inv_rms = lax.rsqrt(square_sum / DM + 1e-06)
    hidden_local = lax.dynamic_slice_in_dim(hidden_sum, offset, slice_width, 1)
    normed = (hidden_sum * inv_rms[:, None]).astype(jnp.bfloat16)
    outgoing = jnp.dot(placement, normed, preferred_element_type=jnp.float32).astype(jnp.bfloat16)
    outgoing = outgoing.reshape(experts_total, CAP, normed.shape[1])
    incoming = dispatch(outgoing, n_dp, 2)
    up_sum = jnp.dot(
        incoming.reshape(-1, incoming.shape[2]), up_rows, preferred_element_type=jnp.float32
    )
    hidden = jax.nn.silu(up_sum).astype(jnp.bfloat16)
    down_rows = down_weight[0]
    returned = combine(hidden, down_rows, n_tensor, n_dp, 3)
    chosen = expert_ids[:, :, None] == jnp.arange(experts_total, dtype=jnp.int32)
    chosen_logit = (
        jnp.sum(jnp.where(chosen, raw_logits[:, None, :], 0.0), axis=2) * inv_rms[:, None]
    )
    first = 1.0 / (1.0 + jnp.exp(chosen_logit[:, 1] - chosen_logit[:, 0]))
    second = 1.0 / (1.0 + jnp.exp(chosen_logit[:, 0] - chosen_logit[:, 1]))
    route_weight = jnp.stack([first, second], axis=1) * live_float[:, None]
    mix = jnp.sum(
        jnp.where(buffer_row[:, :, None] == row_numbers, route_weight[:, :, None], 0.0), axis=1
    )
    expert_sum = jnp.dot(
        mix,
        returned.reshape(-1, slice_width).astype(jnp.float32),
        precision=lax.Precision.HIGHEST,
    )
    layer_out = (hidden_local + expert_sum).astype(jnp.bfloat16)
    return (layer_out, state_out, conv_cache)


def solution(mesh):
    placed = (
        P("dp", "tensor"),
        P("dp", "tensor"),
        P("dp", None, "tensor"),
        P(None, "tensor"),
        P("tensor"),
        P("tensor", None),
        P(None, "tensor"),
        P("tensor"),
        P(None, "tensor"),
        P("tensor"),
        P("dp", None, "tensor"),
        P("tensor", None),
        P("dp", "tensor"),
        P(),
        P("dp", None),
        P("dp"),
        P("dp", None, "tensor"),
        P("dp", "tensor", None),
    )
    return jax.shard_map(
        functools.partial(local, mesh.shape["tensor"], mesh.shape["dp"]),
        mesh=mesh,
        in_specs=placed,
        out_specs=(P("dp", "tensor"), P("dp", None, "tensor"), P("dp", None, "tensor")),
        check_vma=False,
    )
```
